256 devices in a mesh: req: 32 (over x, z_hi, core), ctx: 8 (over z_lo, y).
Axes of the slice: x: 4, y: 4, z: 8 (z_hi: 4, z_lo: 2; z = z_hi * 2 + z_lo), core: 2. Of those that a mesh axis runs over, the one named last changes fastest.
Arguments:
- q_heads: bfloat16 [32, 1024, 12288], P('req', 'ctx'), may hold values from -204 to 204
- kv_latent: bfloat16 [32, 1024, 576], P('req', 'ctx'), may hold values from -600 to 600
- latent_gain: float32 [512], replicated, may hold values from 0.1 to 1.9
- kv_up: bfloat16 [64, 256, 512], P('ctx'), may hold values from -0.25 to 0.25
- offsets: int32 [32], P('req'), may hold values from 0 to 7168, as said below
- lengths: int32 [32], P('req'), may hold values from 64 to 1024
- block_order: int32 [32, 16], P('req'), may hold values from 0 to 15, each once within a row
- owners: int32 [32, 16], P(None, 'ctx'), may hold values from 0 to 31, as said below
Outputs:
- attn_out: bfloat16 [32, 1024, 8192], P('req', 'ctx')
- shipped: bfloat16 [32, 16, 36864], P('req', 'ctx')
The draws below stay inside these ranges and needn't reach their ends.
Inputs may be any that keep to these rules, and one draw needn't show every extreme that they name: `offsets`: each entry is a multiple of 1024. `block_order`: each row names every block index once. `owners`: for each context index j, column 2 j and column 2 j + 1 each name every owner once, and no row names the same owner in both of them.
All inputs are finite; a program needn't handle non-finite values.
Results may differ from the reference program's by a relative error of at most 0.007.
Values may be sent and summed in bfloat16 or wider, within the bound.
No kernel may reach another device: no remote copies, remote signals or barrier semaphores. Data moves between devices by JAX's collectives and lax.ppermute only.
A program may use at most 64 MiB of HBM per device.

```python
import math
import jax
import jax.numpy as jnp
from jax import lax

HEADS = 64
HD = 128
ROPE = 64
LAT = 512
SEGMENTS = 8
BLK = 64
SEGLEN = 1024
REQS = 32
KVW = 576
N_CTX = 8


def draw_q_heads(key, part):
    subkeys = jax.random.split(key, 1)
    shape_full = (REQS, SEGLEN, HEADS * (HD + ROPE))
    values = jnp.clip(jax.random.normal(subkeys[0], shape_full, jnp.float32), -6.0, 6.0)
    return values.astype(jnp.bfloat16)


def draw_kv_latent(key, part):
    subkeys = jax.random.split(key, 5)
    shape_latent = (REQS, SEGLEN, LAT)
    row_scale = jnp.exp(jax.random.uniform(subkeys[0], (REQS, SEGLEN, 1), jnp.float32, 0.0, math.log(10.0)))
    column_scale = jnp.exp(jax.random.uniform(subkeys[1], (1, 1, LAT), jnp.float32, 0.0, math.log(10.0)))
    latent = jnp.clip(jax.random.normal(subkeys[3], shape_latent, jnp.float32), -6.0, 6.0) * row_scale * column_scale
    rope_part = jnp.clip(jax.random.normal(subkeys[4], (REQS, SEGLEN, ROPE), jnp.float32), -6.0, 6.0)
    values = jnp.clip(jnp.concatenate([latent, rope_part], axis=-1), -600.0, 600.0)
    return values.astype(jnp.bfloat16)


def draw_offsets(key, part):
    subkeys = jax.random.split(key, 2)
    values = SEGLEN * jax.random.randint(subkeys[0], (REQS,), 0, SEGMENTS)
    picked = jax.random.permutation(subkeys[1], REQS)
    values = values.at[picked[0]].set(0).at[picked[1]].set((SEGMENTS - 1) * SEGLEN)
    return values.astype(jnp.int32)


def draw_lengths(key, part):
    subkeys = jax.random.split(key, 2)
    values = jax.random.randint(subkeys[0], (REQS,), BLK, SEGLEN + 1)
    picked = jax.random.permutation(subkeys[1], REQS)
    values = values.at[picked[0]].set(SEGLEN).at[picked[1]].set(BLK)
    return values.astype(jnp.int32)


def draw_owners(key, part):
    columns = []
    for context in range(N_CTX):
        subkeys = jax.random.split(jax.random.fold_in(key, 7 + context), 2)
        first_owner = jax.random.permutation(subkeys[0], REQS).astype(jnp.int32)
        shift_by = jax.random.randint(subkeys[1], (), 1, REQS)
        second_owner = first_owner[(jnp.arange(REQS, dtype=jnp.int32) + shift_by) % REQS]
        columns.append(first_owner)
        columns.append(second_owner)
    return jnp.stack(columns, axis=1).astype(jnp.int32)


def block_levels(own_key, extent, cuts, low, high):
    factor_of, own = 1.0, jax.random.fold_in(own_key, 6)
    for axis_at, blocks in cuts:
        draws = jnp.exp(jax.random.uniform(jax.random.fold_in(own, axis_at), (blocks,), jnp.float32, low / len(cuts), high / len(cuts)))
        factor_of = factor_of * jnp.repeat(draws, extent[axis_at] // blocks).reshape([-1 if axis == axis_at else 1 for axis in range(len(extent))])
    return factor_of


def bell_draw(key, shape, deviation, reach, cuts=(), held_as=jnp.bfloat16):
    loudness = block_levels(key, shape, cuts, -0.22, 0.18) if cuts else 1.0
    entries = jax.random.normal(key, shape, jnp.float32) * deviation * loudness
    return jnp.minimum(jnp.maximum(entries, -reach), reach).astype(held_as)


def setup_inputs(seed: int = 0) -> dict:
    key_list = jax.random.split(jax.random.key(seed), 9)
    return {
        "q_heads": draw_q_heads(jax.random.fold_in(key_list[8], 71), 0),
        "kv_latent": draw_kv_latent(jax.random.fold_in(key_list[8], 71), 0),
        "latent_gain": jnp.clip(1.0 + 0.18 * jax.random.normal(key_list[2], (LAT,), jnp.float32), 0.1, 1.9),
        "kv_up": bell_draw(key_list[3], (HEADS, 2 * HD, LAT), LAT ** -0.5, 0.25, ((0, 8),)),
        "offsets": draw_offsets(jax.random.fold_in(key_list[8], 71), 0),
        "lengths": draw_lengths(jax.random.fold_in(key_list[8], 71), 0),
        "block_order": jax.vmap(lambda own: jax.random.permutation(own, 2 * N_CTX))(jax.random.split(key_list[6], REQS)).reshape((REQS, 2 * N_CTX)).astype(jnp.int32),
        "owners": draw_owners(jax.random.fold_in(key_list[8], 71), 0),
    }


theta_base = 10000.0
epsilon = 1e-06
masked_fill = -1e+30

def rotate(values, angles):
    half_width = values.shape[-1] // 2
    first_half = values[..., :half_width]
    second_half = values[..., half_width:]
    cosine = jnp.cos(angles)
    sine_part = jnp.sin(angles)
    return jnp.concatenate([first_half * cosine - second_half * sine_part, second_half * cosine + first_half * sine_part], axis=-1)

def angle_table(positions, rope_width):
    half_width = rope_width // 2
    frequency = jnp.exp(-math.log(theta_base) * jnp.arange(half_width, dtype=jnp.float32) / half_width)
    return positions.astype(jnp.float32)[:, None] * frequency[None, :]

def make_cache(latent_rows, latent_gain, angles):
    latent = latent_rows[:, :LAT].astype(jnp.float32)
    mean_square = lax.optimization_barrier(jnp.mean(latent * latent, axis=-1, keepdims=True))
    normed = (latent * lax.rsqrt(mean_square + epsilon) * latent_gain).astype(jnp.bfloat16)
    key_rope = rotate(latent_rows[:, LAT:].astype(jnp.float32), angles).astype(jnp.bfloat16)
    return jnp.concatenate([normed, key_rope], axis=-1)

def attend(queries, key_rows, value_weight, allowed, valid_rows):
    score_scale = (HD + ROPE) ** (-0.5)
    scores = jnp.dot(queries, key_rows.T, preferred_element_type=jnp.float32) * score_scale
    masked = jnp.where(allowed, scores, masked_fill)
    row_max = lax.optimization_barrier(jnp.max(masked, axis=-1, keepdims=True))
    exponent = jnp.exp(masked - row_max)
    probabilities = (exponent / lax.optimization_barrier(jnp.sum(exponent, axis=-1, keepdims=True))).astype(jnp.bfloat16)
    output_latent = jnp.dot(probabilities, key_rows[:, :LAT], preferred_element_type=jnp.float32).astype(jnp.bfloat16)
    projected = jnp.dot(output_latent, value_weight.T, preferred_element_type=jnp.float32)
    return jnp.where(valid_rows[:, None], projected, 0.0).astype(jnp.bfloat16)

def reference(q_heads, kv_latent, latent_gain, kv_up, offsets, lengths, block_order, owners):
    segment_rows = jnp.arange(SEGLEN, dtype=jnp.int32)

    def one_request(request):
        positions = block_order[request][segment_rows // BLK] * BLK + segment_rows % BLK
        angles = angle_table(offsets[request] + positions, ROPE)
        cache_rows = make_cache(kv_latent[request], latent_gain, angles)
        query_parts = q_heads[request].reshape(SEGLEN, HEADS, HD + ROPE)
        query_rope = rotate(query_parts[:, :, HD:].astype(jnp.float32), angles[:, None, :]).astype(jnp.bfloat16)
        allowed = (positions[None, :] <= positions[:, None]) & (positions[None, :] < lengths[request])
        valid_rows = positions < lengths[request]

        def one_head(head_index):
            weight = kv_up[head_index]
            query_latent = jnp.dot(query_parts[:, head_index, :HD], weight[:HD], preferred_element_type=jnp.float32).astype(jnp.bfloat16)
            queries = jnp.concatenate([query_latent, query_rope[:, head_index]], axis=-1)
            return attend(queries, cache_rows, weight[HD:], allowed, valid_rows)
        per_head = lax.map(one_head, jnp.arange(HEADS, dtype=jnp.int32))
        return (per_head.transpose(1, 0, 2).reshape(SEGLEN, HEADS * HD), cache_rows)
    attn_out, caches = lax.map(one_request, jnp.arange(REQS, dtype=jnp.int32))
    page_rows = caches.reshape(REQS, N_CTX, 2, BLK * KVW)
    source_index = jnp.arange(2 * REQS, dtype=jnp.int32)
    owner_index = jnp.arange(REQS, dtype=jnp.int32)
    columns = []
    for context in range(N_CTX):
        named_owner = owners[:, 2 * context:2 * context + 2].reshape(2 * REQS)
        matches = named_owner[None, :] == owner_index[:, None]
        first_slot = lax.optimization_barrier(jnp.min(jnp.where(matches, source_index[None, :], 2 * REQS), axis=1))
        second_slot = lax.optimization_barrier(jnp.min(jnp.where(matches & (source_index[None, :] != first_slot[:, None]), source_index[None, :], 2 * REQS), axis=1))
        candidates = page_rows[:, context].reshape(2 * REQS, BLK * KVW)
        columns.append(jnp.stack([candidates[first_slot], candidates[second_slot]], axis=1))
    shipped = jnp.stack(columns, axis=1).reshape(REQS, N_CTX * 2, BLK * KVW)
    return (attn_out, shipped)
```

```python
import functools
import math

import jax
import jax.numpy as jnp
from jax import lax
from jax.experimental import pallas as pl
from jax.experimental.pallas import tpu as pltpu
from jax.sharding import PartitionSpec as P


HEADS = 64
HD = 128
ROPE = 64
LAT = 512
QW = HD + ROPE
PAIR = 2 * QW
BLK = 64
TILE = 256
GROUPS = 8
LOCAL = 2 * BLK
KVP = LAT + 128
PAGE = BLK * (LAT + ROPE) // 128

CHUNKS = 2
PAIRS = 4 // CHUNKS
QPART = PAIRS * PAIR
OPART = PAIRS * 2 * HD

theta_base = 10000.0
epsilon = 1e-06
masked_fill = -1e30
log2_scale = math.log2(math.e) * QW ** (-0.5)


NT = (((1,), (1,)), ((), ()))
SMEM = pl.BlockSpec(memory_space=pltpu.SMEM)
VMEM = pl.BlockSpec(memory_space=pltpu.VMEM)
ANY = pl.BlockSpec(memory_space=pl.ANY)

OFFSETS = ((0, 0), (0, 1), (0, 3), (1, 0), (1, 1), (1, 3), (0, 2), (1, 2))
BESIDE = {1: 4, 2: 5, 6: 7}
EARLY, LATE = (7, 4, 5, 3), (6, 1, 2)


def partner(context, k, back=False):
    dz, dy = OFFSETS[k]
    z, y = context // 4, context % 4
    step = 4 - dy if back else dy
    return ((z + dz) % 2) * 4 + (y + step) % 4


def forward(k):
    return [(d, partner(d, k)) for d in range(GROUPS)]


def params(limit):
    return pltpu.CompilerParams(vmem_limit_bytes=limit << 20)


def angle_table(positions):
    half = ROPE // 2
    frequency = jnp.exp(-math.log(theta_base) * jnp.arange(half, dtype=jnp.float32) / half)
    return positions.astype(jnp.float32)[:, None] * frequency[None, :]


def rotate_lanes(x, cosine, sine, lane):
    half = ROPE // 2
    swapped = jnp.where(lane % ROPE < half, pltpu.roll(x, 128 - half, 1), pltpu.roll(x, half, 1))
    return x * cosine + swapped * sine


def pack_kernel(chunk, partners, n_kv, *refs):
    ctx_ref, q_ref, *refs = refs
    kvs, refs = refs[:n_kv], refs[n_kv:]
    outs, (held, sems) = refs[: len(partners)], refs[len(partners) :]
    loads, stores = [], []
    for n, k in enumerate(partners):
        column = partner(ctx_ref[0], k) * (4 * PAIR) + chunk * QPART
        columns = pl.ds(pl.multiple_of(column, 128), QPART)
        loads.append(pltpu.make_async_copy(q_ref.at[0, :, columns], held.at[n], sems.at[0, n]))
        loads[-1].start()
    for n in range(len(partners)):
        for i, kv in enumerate(kvs):
            columns = pl.ds(QPART + i * KVP, KVP)
            stores.append(pltpu.make_async_copy(kv, outs[n].at[:, columns], sems.at[2 + i, n]))
            stores[-1].start()
    for n in range(len(partners)):
        loads[n].wait()
        stores.append(pltpu.make_async_copy(held.at[n], outs[n].at[:, :QPART], sems.at[1, n]))
        stores[-1].start()
    for store in stores:
        store.wait()


def pack(context, q_heads, chunk, partners, kvs=()):
    count = len(partners)
    outs = pl.pallas_call(
        functools.partial(pack_kernel, chunk, partners, len(kvs)),
        in_specs=[SMEM, ANY] + [VMEM] * len(kvs),
        out_specs=[ANY] * count,
        out_shape=[jax.ShapeDtypeStruct((LOCAL, QPART + len(kvs) * KVP), jnp.bfloat16)] * count,
        scratch_shapes=[
            pltpu.VMEM((count, LOCAL, QPART), jnp.bfloat16),
            pltpu.SemaphoreType.DMA((4, count)),
        ],
        compiler_params=params(8),
        name="pack",
    )(context, q_heads, *kvs)
    return dict(zip(partners, outs))


def pack_all_kernel(chunk, q_ref, o_ref, held, sems):
    loads, stores = [], []
    for j in range(GROUPS):
        columns = pl.ds(j * (4 * PAIR) + chunk * QPART, QPART)
        loads.append(pltpu.make_async_copy(q_ref.at[0, :, columns], held.at[j], sems.at[0, j]))
        loads[-1].start()
    for j in range(GROUPS):
        loads[j].wait()
        stores.append(pltpu.make_async_copy(held.at[j], o_ref.at[j], sems.at[1, j]))
        stores[-1].start()
    for store in stores:
        store.wait()


def pack_all(chunk, q_heads):
    shape = (GROUPS, LOCAL, QPART)
    return pl.pallas_call(
        functools.partial(pack_all_kernel, chunk),
        in_specs=[ANY],
        out_specs=ANY,
        out_shape=jax.ShapeDtypeStruct(shape, jnp.bfloat16),
        scratch_shapes=[pltpu.VMEM(shape, jnp.bfloat16), pltpu.SemaphoreType.DMA((2, GROUPS))],
        compiler_params=params(8),
        name="pack_all",
    )(q_heads)


def attend_kernel(first, *refs):
    ctx_ref, order_ref, length_ref, *refs = refs
    if first:
        arrived, refs = refs[:GROUPS], refs[GROUPS:]
        w_ref, cosines_ref, sines_ref, gain_ref, kv_ref, kvz_ref, o_ref, cs, krl, *refs = refs
    else:
        stacked, w_ref, cosines_ref, sines_ref, cs, krl, o_ref, *refs = refs
        arrived = [stacked.at[k] for k in range(GROUPS)]
    krr, cos_ref, sin_ref, *refs = refs
    qs, os, k0, k1, v = refs
    total = cs.shape[0]
    context = ctx_ref[0]

    if first:
        rows_of = {0: (kv_ref, 0), 3: (kvz_ref, 0)}
        for k, beyond in BESIDE.items():
            rows_of[k] = (arrived[k], QPART)
            rows_of[beyond] = (arrived[k], QPART + KVP)
    places = []
    for k in range(GROUPS):
        source = partner(context, k, back=True) if first else k
        for i in range(2):
            place = pl.multiple_of(order_ref[2 * source + i] * BLK, BLK)
            places.append((2 * source + i, place))
            here, there = slice(i * BLK, (i + 1) * BLK), pl.ds(place, BLK)
            for pair in range(PAIRS):
                qs[pair, there, :] = arrived[k][here, pair * PAIR : (pair + 1) * PAIR]
            if first:
                ref, at = rows_of[k]
                cs[there, :] = ref[here, at : at + LAT]
                krl[there, :] = ref[here, at + LAT : at + KVP]

    lane = lax.broadcasted_iota(jnp.int32, (TILE, 128), 1)
    for t in range(total // TILE):
        rows = slice(t * TILE, (t + 1) * TILE)
        cosine, sine = cosines_ref[:, rows].T, sines_ref[:, rows].T
        cosine = jnp.concatenate([cosine] * 4, axis=1)
        sine = jnp.concatenate([-sine, sine] * 2, axis=1)
        cos_ref[rows, :] = cosine
        sin_ref[rows, :] = sine
        if first:
            latent = cs[rows, :].astype(jnp.float32)
            mean_square = jnp.mean(latent * latent, axis=-1, keepdims=True)
            cs[rows, :] = (latent * lax.rsqrt(mean_square + epsilon) * gain_ref[...]).astype(jnp.bfloat16)
            turned = rotate_lanes(krl[rows, :].astype(jnp.float32), cosine, sine, lane)
            krl[rows, :] = turned.astype(jnp.bfloat16)
        else:
            turned = krl[rows, :].astype(jnp.float32)
        krr[rows, :] = pltpu.roll(turned, ROPE, 1).astype(jnp.bfloat16)

    length = length_ref[0]

    @pl.loop(0, PAIRS)
    def _(pair):
        gap = jnp.zeros((ROPE, LAT), jnp.bfloat16)
        w0, w1 = w_ref[2 * pair], w_ref[2 * pair + 1]
        wk = jnp.concatenate([w0[:HD], gap, w1[:HD], gap], axis=0)
        wv = jnp.concatenate([w0[HD:], w1[HD:]], axis=0)
        for t in range(total // TILE):
            rows = slice(t * TILE, (t + 1) * TILE)
            cache = cs[rows, :]
            kn = lax.dot_general(cache, wk, NT, preferred_element_type=jnp.float32).astype(jnp.bfloat16)
            k0[rows, :128] = kn[:, :128]
            k0[rows, 128:] = krl[rows, :]
            k1[rows, :128] = kn[:, 128:256]
            k1[rows, 128:] = kn[:, 256:] + krr[rows, :]
            v[rows, :] = lax.dot_general(cache, wv, NT, preferred_element_type=jnp.float32).astype(jnp.bfloat16)
        for t in range(total // TILE):
            rows = slice(t * TILE, (t + 1) * TILE)
            keys = (t + 1) * TILE
            cosine, sine = cos_ref[rows, :], sin_ref[rows, :]
            one = qs[pair, rows, 128:256].astype(jnp.float32)
            two = qs[pair, rows, 256:].astype(jnp.float32)
            one = jnp.where(lane < ROPE, rotate_lanes(one, cosine, sine, lane), one).astype(jnp.bfloat16)
            two = jnp.where(lane < ROPE, two, rotate_lanes(two, cosine, sine, lane)).astype(jnp.bfloat16)
            queries = (jnp.concatenate([qs[pair, rows, :128], one], axis=1), jnp.concatenate([one, two], axis=1))
            row = lax.broadcasted_iota(jnp.int32, (TILE, TILE), 0)
            column = lax.broadcasted_iota(jnp.int32, (TILE, TILE), 1)
            valid = lax.broadcasted_iota(jnp.int32, (TILE, HD), 0) + t * TILE < length
            for head, k in ((0, k0), (1, k1)):
                s = lax.dot_general(queries[head], k[:keys, :], NT, preferred_element_type=jnp.float32)
                last = jnp.where(column <= row, s[:, keys - TILE :], masked_fill)
                s = last if t == 0 else jnp.concatenate([s[:, : keys - TILE], last], axis=1)
                top = jnp.max(s, axis=1, keepdims=True)
                p = jnp.exp2((s - top) * log2_scale)
                bottom = jnp.sum(p, axis=1, keepdims=True)
                side = slice(head * HD, (head + 1) * HD)
                o = jnp.dot(p.astype(jnp.bfloat16), v[:keys, side], preferred_element_type=jnp.float32)
                os[pair, rows, side] = jnp.where(valid, o / bottom, 0.0).astype(jnp.bfloat16)

    for block, place in places:
        for pair in range(PAIRS):
            o_ref[block, :, pair * 2 * HD : (pair + 1) * 2 * HD] = os[pair, pl.ds(place, BLK), :]


def attend(chunk, context, order_row, length, arrived, kv_up, extra):
    first = chunk == 0
    total = GROUPS * LOCAL
    whole = lambda a: pl.BlockSpec(a.shape, lambda i: (0,) * a.ndim)
    out = jax.ShapeDtypeStruct((2 * GROUPS, BLK, OPART), jnp.bfloat16)
    kept = [((total, LAT), jnp.bfloat16), ((total, 128), jnp.bfloat16)]
    outs = [out] + [jax.ShapeDtypeStruct(*one) for one in kept] * first
    outs = pl.pallas_call(
        functools.partial(attend_kernel, first),
        grid=(1,),
        in_specs=[SMEM, SMEM, SMEM]
        + [whole(a) for a in arrived]
        + [pl.BlockSpec((2 * PAIRS, 2 * HD, LAT), lambda i: (chunk, 0, 0))]
        + [whole(a) for a in extra],
        out_specs=[whole(a) for a in outs],
        out_shape=outs,
        scratch_shapes=[
            pltpu.VMEM((total, 128), jnp.bfloat16),
            pltpu.VMEM((total, 128), jnp.float32),
            pltpu.VMEM((total, 128), jnp.float32),
            pltpu.VMEM((PAIRS, total, PAIR), jnp.bfloat16),
            pltpu.VMEM((PAIRS, total, 2 * HD), jnp.bfloat16),
            pltpu.VMEM((total, 256), jnp.bfloat16),
            pltpu.VMEM((total, 256), jnp.bfloat16),
            pltpu.VMEM((total, 256), jnp.bfloat16),
        ],
        compiler_params=params(60),
        cost_estimate=pl.CostEstimate(
            flops=PAIRS * 2_200_000_000, bytes_accessed=6_000_000, transcendentals=PAIRS * 1_300_000
        ),
        name="attend",
    )(context, order_row, length, *arrived, kv_up, *extra)
    return outs[0].reshape(GROUPS, LOCAL, OPART), outs[1:]


def unpack_kernel(chunk, part_ref, *refs):
    o_ref, sems = refs[-2:]
    stores = []
    for j in range(GROUPS):
        columns = pl.ds(j * (8 * HD) + chunk * OPART, OPART)
        stores.append(pltpu.make_async_copy(part_ref.at[j], o_ref.at[0, :, columns], sems.at[j]))
        stores[-1].start()
    for store in stores:
        store.wait()


def unpack(chunk, part, out):
    more = [] if out is None else [out]
    return pl.pallas_call(
        functools.partial(unpack_kernel, chunk),
        in_specs=[VMEM] + [ANY] * len(more),
        out_specs=ANY,
        out_shape=jax.ShapeDtypeStruct((1, LOCAL, HEADS * HD), jnp.bfloat16),
        scratch_shapes=[pltpu.SemaphoreType.DMA((GROUPS,))],
        input_output_aliases={1: 0} if more else {},
        compiler_params=params(8),
        name="unpack",
    )(part, *more)


def pages_kernel(ctx_ref, order_ref, offset_ref, kv_ref, gain_ref, freq_ref, o_ref, rows, page):
    row = lax.broadcasted_iota(jnp.int32, (LOCAL, 128), 0)
    lane = lax.broadcasted_iota(jnp.int32, (LOCAL, 128), 1)
    first, second = order_ref[2 * ctx_ref[0]], order_ref[2 * ctx_ref[0] + 1]
    position = jnp.where(row < BLK, first, second) * BLK + row % BLK + offset_ref[0]
    angles = position.astype(jnp.float32) * freq_ref[...]
    sine = jnp.sin(angles)
    latent = kv_ref[:, :LAT].astype(jnp.float32)
    mean_square = jnp.mean(latent * latent, axis=-1, keepdims=True)
    normed = latent * lax.rsqrt(mean_square + epsilon) * gain_ref[...]
    for t in range(4):
        rows[t] = normed[:, 128 * t : 128 * (t + 1)].astype(jnp.bfloat16).astype(jnp.float32)
    rope = kv_ref[:, LAT:].astype(jnp.float32)
    rope = rotate_lanes(rope, jnp.cos(angles), jnp.where(lane % ROPE < ROPE // 2, -sine, sine), lane)
    rows[4] = rope.astype(jnp.bfloat16).astype(jnp.float32)
    half = BLK // 2
    left = lax.broadcasted_iota(jnp.int32, (half, 128), 1) < ROPE
    for i in range(2):
        even = [rows[t, pl.ds(i * BLK, half, stride=2), :] for t in range(5)]
        odd = [pltpu.roll(rows[t, pl.ds(i * BLK + 1, half, stride=2), :], ROPE, 1) for t in range(5)]
        for t in range(9):
            if t < 4:
                tile = even[t]
            elif t == 4:
                tile = jnp.where(left, even[4], odd[0])
            else:
                tile = jnp.where(left, odd[t - 5], odd[t - 4])
            page[pl.ds(t, half, stride=9), :] = tile
        o_ref[i] = page[...].astype(jnp.bfloat16)


def make_pages(context, order_row, offsets, kv, gain):
    half = ROPE // 2
    lane = jnp.arange(128) % half
    freq = jnp.exp(-math.log(theta_base) * lane.astype(jnp.float32) / half)
    return pl.pallas_call(
        pages_kernel,
        in_specs=[SMEM] * 3 + [VMEM] * 3,
        out_specs=VMEM,
        out_shape=jax.ShapeDtypeStruct((2, PAGE, 128), jnp.bfloat16),
        scratch_shapes=[pltpu.VMEM((5, LOCAL, 128), jnp.float32), pltpu.VMEM((PAGE, 128), jnp.float32)],
        compiler_params=params(8),
        name="pages",
    )(context, order_row, offsets, kv, gain, freq[None])


def merge_kernel(one_ref, two_ref, o_ref):
    o_ref[:2] = one_ref[...]
    o_ref[2:] = two_ref[...]


def merge(one, two):
    return pl.pallas_call(
        merge_kernel,
        in_specs=[VMEM] * 2,
        out_specs=VMEM,
        out_shape=jax.ShapeDtypeStruct((4, PAGE, 128), jnp.bfloat16),
        compiler_params=params(8),
        name="merge",
    )(one, two)


def relay_kernel(req_ref, owners_ref, table_ref, *refs):
    parts, (o_ref, final_ref, table, count, sems) = refs[:4], refs[4:]
    me = req_ref[0]
    my_x, my_z, my_core = me // 8, (me // 2) % 4, me % 2
    for i in range(8):
        table[i] = 0
    for i in range(4):
        count[i] = 0
    for x in range(4):
        back = (my_x + 4 - x) % 4
        for core in range(2):
            for page in range(2):
                owner = owners_ref[page, request(x, my_z, core)]

                @pl.when((owner // 8 == my_x) & (owner % 2 == my_core))
                def _():
                    turn = ((owner // 2) % 4 + 4 - my_z) % 4
                    slot = count[turn]
                    table[2 * turn + jnp.minimum(slot, 1)] = 4 * back + 2 * (core ^ my_core) + page
                    count[turn] = slot + 1

    for i in range(8):
        for d, part in enumerate(parts):

            @pl.when(table[i] // 4 == d)
            def _():
                pltpu.make_async_copy(part.at[table[i] % 4], o_ref.at[i], sems.at[i]).start()

    owner = table_ref[...]
    flat = 2 * lax.broadcasted_iota(jnp.int32, owner.shape, 1) + lax.broadcasted_iota(jnp.int32, owner.shape, 0)
    first = jnp.min(jnp.where(owner == me, flat, 4 * owner.shape[1]))
    last = jnp.max(jnp.where(owner == me, flat, 0))
    first = jnp.minimum(first, last)
    turn_first = (my_z + 4 - (first // 4) % 4) % 4
    turn_last = (my_z + 4 - (last // 4) % 4) % 4
    final_ref[0] = 2 * turn_first
    final_ref[1] = 2 * turn_last + jnp.where(turn_first == turn_last, 1, 0)
    for i in range(8):
        pltpu.make_async_copy(parts[0].at[0], o_ref.at[i], sems.at[i]).wait()


def relay_pages(req, owners, parts):
    page = parts[0].shape[1:]
    return pl.pallas_call(
        relay_kernel,
        in_specs=[SMEM, SMEM, VMEM] + [ANY] * 4,
        out_specs=[VMEM, SMEM],
        out_shape=[
            jax.ShapeDtypeStruct((8,) + page, parts[0].dtype),
            jax.ShapeDtypeStruct((2,), jnp.int32),
        ],
        scratch_shapes=[
            pltpu.SMEM((8,), jnp.int32),
            pltpu.SMEM((4,), jnp.int32),
            pltpu.SemaphoreType.DMA((8,)),
        ],
        compiler_params=params(8),
        name="relay_pages",
    )(req, owners, owners, *parts)


def keep_kernel(final_ref, *refs):
    o_ref = refs[-1]
    for i in range(2):
        for turn, ref in enumerate(refs[:-1]):

            @pl.when(final_ref[i] // 2 == turn)
            def _():
                o_ref[i] = ref[final_ref[i] % 2]


def keep_pages(final, parts):
    return pl.pallas_call(
        keep_kernel,
        in_specs=[SMEM] + [VMEM] * len(parts),
        out_specs=VMEM,
        out_shape=jax.ShapeDtypeStruct(parts[0].shape, parts[0].dtype),
        compiler_params=params(8),
        name="keep_pages",
    )(final, *parts)


def request(x, z, core):
    return (x * 4 + z) * 2 + core


EACH = [(x, z, c) for x in range(4) for z in range(4) for c in range(2)]


def along_x(d):
    return [(request(x, z, c), request((x + d) % 4, z, c)) for x, z, c in EACH]


def along_z(d):
    return [(request(x, z, c), request(x, (z + d) % 4, c)) for x, z, c in EACH]


def ship(pages, owners):
    other = lax.ppermute(pages, "req", [(request(x, z, c), request(x, z, 1 - c)) for x, z, c in EACH])
    both = merge(pages, other)
    parts = [both] + [None] * 3
    for d in (1, 3, 2):
        parts[d] = lax.ppermute(both, "req", along_x(d))
    outgoing, final = relay_pages(lax.axis_index("req").reshape(1), owners.T, parts)
    arrived = [outgoing[:2]] + [lax.ppermute(outgoing[2 * d : 2 * d + 2], "req", along_z(d)) for d in (1, 2, 3)]
    return keep_pages(final, arrived)


def exchange(array):
    return lax.all_to_all(array, "ctx", split_axis=0, concat_axis=0, tiled=True)


def body(q_heads, kv_latent, latent_gain, kv_up, offsets, lengths, block_order, owners):
    context = lax.axis_index("ctx").reshape(1)
    order_row = block_order[0]
    gain = latent_gain[None]
    padded = jnp.pad(kv_latent[0], ((0, 0), (0, KVP - kv_latent.shape[2])))
    beyond = lax.ppermute(padded, "ctx", forward(3))

    sent = pack(context, q_heads, 0, (0,) + EARLY)
    pages = make_pages(context, order_row, offsets, padded, gain)
    shipped = ship(pages, owners).reshape(1, 2, PAGE * 128)
    sent.update(pack(context, q_heads, 0, LATE, (padded, beyond)))
    arrived = [[sent[0]] + [lax.ppermute(sent[k], "ctx", forward(k)) for k in range(1, GROUPS)]]
    for chunk in range(1, CHUNKS):
        arrived.append([exchange(pack_all(chunk, q_heads))])
    offsets, _ = lax.optimization_barrier((offsets, sent[1]))
    angles = angle_table(offsets[0] + jnp.arange(GROUPS * LOCAL, dtype=jnp.int32)).T
    extra = [jnp.cos(angles), jnp.sin(angles), gain, padded, beyond]
    attn_out = None
    for chunk in range(CHUNKS):
        out, kept = attend(chunk, context, order_row, lengths, arrived[chunk], kv_up, extra)
        extra = extra[:2] + list(kept) if chunk == 0 else extra
        attn_out = unpack(chunk, exchange(out), attn_out)
    return attn_out, shipped


def solution(mesh):
    in_specs = (
        P("req", "ctx", None),
        P("req", "ctx", None),
        P(),
        P("ctx", None, None),
        P("req"),
        P("req"),
        P("req", None),
        P(None, "ctx"),
    )
    out_specs = (P("req", "ctx", None), P("req", "ctx", None))
    return jax.shard_map(body, mesh=mesh, in_specs=in_specs, out_specs=out_specs, check_vma=False)
```

```python
import functools
import math

import jax
import jax.numpy as jnp
from jax import lax
from jax.experimental import pallas as pl
from jax.experimental.pallas import tpu as pltpu
from jax.sharding import PartitionSpec as P


HEADS = 64
HD = 128
ROPE = 64
LAT = 512
QW = HD + ROPE
PAIR = 2 * QW
BLK = 64
TILE = 256
GROUPS = 8
LOCAL = 2 * BLK
KVP = LAT + 128
PAGE = BLK * (LAT + ROPE) // 128

CHUNKS = 2
PAIRS = 4 // CHUNKS
QPART = PAIRS * PAIR
OPART = PAIRS * 2 * HD

theta_base = 10000.0
epsilon = 1e-06
masked_fill = -1e30
log2_scale = math.log2(math.e) * QW ** (-0.5)


NT = (((1,), (1,)), ((), ()))
SMEM = pl.BlockSpec(memory_space=pltpu.SMEM)
VMEM = pl.BlockSpec(memory_space=pltpu.VMEM)
ANY = pl.BlockSpec(memory_space=pl.ANY)

OFFSETS = ((0, 0), (0, 1), (0, 3), (1, 0), (1, 1), (1, 3), (0, 2), (1, 2))
BESIDE = {1: 4, 2: 5, 6: 7}
EARLY, LATE = (7, 4, 5, 3), (6, 1, 2)


def partner(context, k, back=False):
    dz, dy = OFFSETS[k]
    z, y = context // 4, context % 4
    step = 4 - dy if back else dy
    return ((z + dz) % 2) * 4 + (y + step) % 4


def forward(k):
    return [(d, partner(d, k)) for d in range(GROUPS)]


def params(limit):
    return pltpu.CompilerParams(vmem_limit_bytes=limit << 20)


def rotate_lanes(x, cosine, sine, lane):
    half = ROPE // 2
    swapped = jnp.where(lane % ROPE < half, pltpu.roll(x, 128 - half, 1), pltpu.roll(x, half, 1))
    return x * cosine + swapped * sine


def pack_kernel(chunk, partners, n_kv, *refs):
    ctx_ref, q_ref, *refs = refs
    kvs, refs = refs[:n_kv], refs[n_kv:]
    outs, (held, sems) = refs[: len(partners)], refs[len(partners) :]
    loads, stores = [], []
    for n, k in enumerate(partners):
        column = partner(ctx_ref[0], k) * (4 * PAIR) + chunk * QPART
        columns = pl.ds(pl.multiple_of(column, 128), QPART)
        loads.append(pltpu.make_async_copy(q_ref.at[0, :, columns], held.at[n], sems.at[0, n]))
        loads[-1].start()
    for n in range(len(partners)):
        for i, kv in enumerate(kvs):
            columns = pl.ds(QPART + i * KVP, KVP)
            stores.append(pltpu.make_async_copy(kv, outs[n].at[:, columns], sems.at[2 + i, n]))
            stores[-1].start()
    for n in range(len(partners)):
        loads[n].wait()
        stores.append(pltpu.make_async_copy(held.at[n], outs[n].at[:, :QPART], sems.at[1, n]))
        stores[-1].start()
    for store in stores:
        store.wait()


def pack(context, q_heads, chunk, partners, kvs=()):
    count = len(partners)
    outs = pl.pallas_call(
        functools.partial(pack_kernel, chunk, partners, len(kvs)),
        in_specs=[SMEM, ANY] + [VMEM] * len(kvs),
        out_specs=[ANY] * count,
        out_shape=[jax.ShapeDtypeStruct((LOCAL, QPART + len(kvs) * KVP), jnp.bfloat16)] * count,
        scratch_shapes=[
            pltpu.VMEM((count, LOCAL, QPART), jnp.bfloat16),
            pltpu.SemaphoreType.DMA((4, count)),
        ],
        compiler_params=params(8 if kvs else 60),
        name="pack",
    )(context, q_heads, *kvs)
    return dict(zip(partners, outs))


def pack_all_kernel(chunk, q_ref, o_ref, held, sems):
    loads, stores = [], []
    for j in range(GROUPS):
        columns = pl.ds(j * (4 * PAIR) + chunk * QPART, QPART)
        loads.append(pltpu.make_async_copy(q_ref.at[0, :, columns], held.at[j], sems.at[0, j]))
        loads[-1].start()
    for j in range(GROUPS):
        loads[j].wait()
        stores.append(pltpu.make_async_copy(held.at[j], o_ref.at[j], sems.at[1, j]))
        stores[-1].start()
    for store in stores:
        store.wait()


def pack_all(chunk, q_heads):
    shape = (GROUPS, LOCAL, QPART)
    return pl.pallas_call(
        functools.partial(pack_all_kernel, chunk),
        in_specs=[ANY],
        out_specs=ANY,
        out_shape=jax.ShapeDtypeStruct(shape, jnp.bfloat16),
        scratch_shapes=[pltpu.VMEM(shape, jnp.bfloat16), pltpu.SemaphoreType.DMA((2, GROUPS))],
        compiler_params=params(60),
        name="pack_all",
    )(q_heads)


def attend_kernel(chunk, *refs):
    first = chunk == 0
    ctx_ref, order_ref, length_ref, *refs = refs
    if first:
        arrived, refs = refs[:GROUPS], refs[GROUPS:]
        w_hbm, cos_hbm, sin_hbm, gain_ref, kv_hbm, kvz_hbm, o_ref, cs_hbm, krl_hbm, krr_hbm, *refs = refs
    else:
        stacked, w_hbm, cos_hbm, sin_hbm, cs_hbm, krl_hbm, krr_hbm, o_ref, *refs = refs
        arrived = [stacked.at[k] for k in range(GROUPS)]
    w_ref, cs, krl, krr, cos_ref, sin_ref, qs, os, k0, k1, v, sems, out_sems = refs
    total = cs.shape[0]
    context = ctx_ref[0]
    started = []

    def load(source, target):
        copy = pltpu.make_async_copy(source, target, sems.at[len(started)])
        copy.start()
        started.append(copy)
        return copy

    rows_of = {}
    if first:
        rows_of = {0: (kv_hbm, 0), 3: (kvz_hbm, 0)}
        for k, beyond in BESIDE.items():
            rows_of[k] = (arrived[k], QPART)
            rows_of[beyond] = (arrived[k], QPART + KVP)
    places, moves = [], []
    for k in range(GROUPS):
        source = partner(context, k, back=True) if first else k
        for i in range(2):
            place = pl.multiple_of(order_ref[2 * source + i] * BLK, BLK)
            places.append((2 * source + i, place))
            moves.append((k, pl.ds(i * BLK, BLK), pl.ds(place, BLK)))
    keys_here = []
    if first:
        for k, here, there in moves:
            ref, at = rows_of[k]
            keys_here.append(load(ref.at[here, pl.ds(at, LAT)], cs.at[there]))
            keys_here.append(load(ref.at[here, pl.ds(at + LAT, KVP - LAT)], krl.at[there]))
    else:
        keys_here = [load(cs_hbm, cs), load(krl_hbm, krl), load(krr_hbm, krr)]
    tables_here = [load(cos_hbm, cos_ref), load(sin_hbm, sin_ref)]
    weights_here, queries_here = [], []
    for pair in range(PAIRS):
        heads = pl.ds(2 * (chunk * PAIRS + pair), 2)
        weights_here.append(load(w_hbm.at[heads], w_ref.at[pl.ds(2 * pair, 2)]))
        queries_here.append(
            [load(arrived[k].at[here, pl.ds(pair * PAIR, PAIR)], qs.at[pair, there]) for k, here, there in moves]
        )
    for copy in keys_here + tables_here * first:
        copy.wait()

    lane = lax.broadcasted_iota(jnp.int32, (TILE, 128), 1)
    if first:
        for t in range(total // TILE):
            rows = slice(t * TILE, (t + 1) * TILE)
            latent = cs[rows, :].astype(jnp.float32)
            mean_square = jnp.mean(latent * latent, axis=-1, keepdims=True)
            cs[rows, :] = (latent * lax.rsqrt(mean_square + epsilon) * gain_ref[...]).astype(jnp.bfloat16)
            turned = rotate_lanes(krl[rows, :].astype(jnp.float32), cos_ref[rows, :], sin_ref[rows, :], lane)
            krl[rows, :] = turned.astype(jnp.bfloat16)
            krr[rows, :] = pltpu.roll(turned, ROPE, 1).astype(jnp.bfloat16)
    kept = [load(cs, cs_hbm), load(krl, krl_hbm), load(krr, krr_hbm)] if first else []
    length = length_ref[0]

    row = lax.broadcasted_iota(jnp.int32, (TILE, TILE), 0)
    column = lax.broadcasted_iota(jnp.int32, (TILE, TILE), 1)
    stores = []

    def project(pair):
        gap = jnp.zeros((ROPE, LAT), jnp.bfloat16)
        w0, w1 = w_ref[2 * pair], w_ref[2 * pair + 1]
        wk = jnp.concatenate([w0[:HD], gap, w1[:HD], gap], axis=0)
        wv = jnp.concatenate([w0[HD:], w1[HD:]], axis=0)
        for t in range(total // TILE):
            rows = slice(t * TILE, (t + 1) * TILE)
            cache = cs[rows, :]
            kn = lax.dot_general(cache, wk, NT, preferred_element_type=jnp.float32).astype(jnp.bfloat16)
            k0[pair, rows, :128] = kn[:, :128]
            k0[pair, rows, 128:] = krl[rows, :]
            k1[pair, rows, :128] = kn[:, 128:256]
            k1[pair, rows, 128:] = kn[:, 256:] + krr[rows, :]
            v[pair, rows, :] = lax.dot_general(cache, wv, NT, preferred_element_type=jnp.float32).astype(jnp.bfloat16)

    def score(pair, t, head):
        rows = slice(t * TILE, (t + 1) * TILE)
        cosine, sine = cos_ref[rows, :], sin_ref[rows, :]
        mixed = qs[pair, rows, 128 * (1 + head) : 128 * (2 + head)].astype(jnp.float32)
        turned = rotate_lanes(mixed, cosine, sine, lane)
        if head == 0:
            mixed = jnp.where(lane < ROPE, turned, mixed).astype(jnp.bfloat16)
            query = jnp.concatenate([qs[pair, rows, :128], mixed], axis=1)
        else:
            mixed = jnp.where(lane < ROPE, mixed, turned).astype(jnp.bfloat16)
            query = jnp.concatenate([qs[pair, rows, 128:256], mixed], axis=1)
        k = (k0, k1)[head]
        last = lax.dot_general(query, k[pair, rows, :], NT, preferred_element_type=jnp.float32)
        last = jnp.where(column <= row, last, masked_fill)
        if t == 0:
            return [last]
        return [lax.dot_general(query, k[pair, : t * TILE, :], NT, preferred_element_type=jnp.float32), last]

    def weigh(pair, t, head, scores):
        rows = slice(t * TILE, (t + 1) * TILE)
        side = slice(head * HD, (head + 1) * HD)
        valid = lax.broadcasted_iota(jnp.int32, (TILE, HD), 0) + t * TILE < length
        top = functools.reduce(jnp.maximum, [jnp.max(s, axis=1, keepdims=True) for s in scores])
        parts = [jnp.exp2((s - top) * log2_scale) for s in scores]
        bottom = functools.reduce(jnp.add, [jnp.sum(p, axis=1, keepdims=True) for p in parts])
        values = [v[pair, : t * TILE, side], v[pair, rows, side]][-len(parts) :]
        o = functools.reduce(
            jnp.add,
            [jnp.dot(p.astype(jnp.bfloat16), u, preferred_element_type=jnp.float32) for p, u in zip(parts, values)],
        )
        os[pair, rows, side] = jnp.where(valid, o / bottom, 0.0).astype(jnp.bfloat16)

    for pair in range(PAIRS):
        weights_here[pair].wait()
        project(pair)
        for copy in queries_here[pair] + tables_here * (not first and pair == 0):
            copy.wait()
        items = [(t, head) for t in range(total // TILE) for head in range(2)]
        ahead = score(pair, *items[0])
        for n, item in enumerate(items):
            scores = ahead
            if n + 1 < len(items):
                ahead = score(pair, *items[n + 1])
            weigh(pair, *item, scores)
        for n, (block, place) in enumerate(places):
            columns = pl.ds(pair * (2 * HD), 2 * HD)
            stores.append(
                pltpu.make_async_copy(
                    os.at[pair, pl.ds(place, BLK)], o_ref.at[block, :, columns], out_sems.at[pair, n]
                )
            )
            stores[-1].start()
    for copy in stores + kept:
        copy.wait()


def attend(chunk, context, order_row, length, arrived, kv_up, extra):
    first = chunk == 0
    total = GROUPS * LOCAL
    shapes = [(2 * GROUPS, BLK, OPART)] + [(total, LAT), (total, 128), (total, 128)] * first
    n_arrived = len(arrived)
    sides = [ANY, ANY, VMEM, ANY, ANY] if first else [ANY] * 5
    outs = pl.pallas_call(
        functools.partial(attend_kernel, chunk),
        in_specs=[SMEM, SMEM, SMEM] + [ANY] * (n_arrived + 1) + sides,
        out_specs=[ANY] * len(shapes),
        out_shape=[jax.ShapeDtypeStruct(shape, jnp.bfloat16) for shape in shapes],
        scratch_shapes=[
            pltpu.VMEM((2 * PAIRS, 2 * HD, LAT), jnp.bfloat16),
            pltpu.VMEM((total, LAT), jnp.bfloat16),
            pltpu.VMEM((total, 128), jnp.bfloat16),
            pltpu.VMEM((total, 128), jnp.bfloat16),
            pltpu.VMEM((total, 128), jnp.float32),
            pltpu.VMEM((total, 128), jnp.float32),
            pltpu.VMEM((PAIRS, total, PAIR), jnp.bfloat16),
            pltpu.VMEM((PAIRS, total, 2 * HD), jnp.bfloat16),
            pltpu.VMEM((PAIRS, total, 256), jnp.bfloat16),
            pltpu.VMEM((PAIRS, total, 256), jnp.bfloat16),
            pltpu.VMEM((PAIRS, total, 256), jnp.bfloat16),
            pltpu.SemaphoreType.DMA((7 + (2 + PAIRS) * 2 * GROUPS,)),
            pltpu.SemaphoreType.DMA((PAIRS, 2 * GROUPS)),
        ],
        compiler_params=params(60),
        cost_estimate=pl.CostEstimate(
            flops=PAIRS * 2_200_000_000, bytes_accessed=6_000_000, transcendentals=PAIRS * 1_300_000
        ),
        name="attend",
    )(context, order_row, length, *arrived, kv_up, *extra)
    return outs[0].reshape(GROUPS, LOCAL, OPART), outs[1:]


def unpack_kernel(chunk, part_ref, *refs):
    o_ref, sems = refs[-2:]
    stores = []
    for j in range(GROUPS):
        columns = pl.ds(j * (8 * HD) + chunk * OPART, OPART)
        stores.append(pltpu.make_async_copy(part_ref.at[j], o_ref.at[0, :, columns], sems.at[j]))
        stores[-1].start()
    for store in stores:
        store.wait()


def unpack(chunk, part, out):
    more = [] if out is None else [out]
    return pl.pallas_call(
        functools.partial(unpack_kernel, chunk),
        in_specs=[VMEM] + [ANY] * len(more),
        out_specs=ANY,
        out_shape=jax.ShapeDtypeStruct((1, LOCAL, HEADS * HD), jnp.bfloat16),
        scratch_shapes=[pltpu.SemaphoreType.DMA((GROUPS,))],
        input_output_aliases={1: 0} if more else {},
        compiler_params=params(8),
        name="unpack",
    )(part, *more)


def pages_kernel(ctx_ref, order_ref, offset_ref, kv_ref, gain_ref, freq_ref, o_ref, rows, page):
    row = lax.broadcasted_iota(jnp.int32, (LOCAL, 128), 0)
    lane = lax.broadcasted_iota(jnp.int32, (LOCAL, 128), 1)
    first, second = order_ref[2 * ctx_ref[0]], order_ref[2 * ctx_ref[0] + 1]
    position = jnp.where(row < BLK, first, second) * BLK + row % BLK + offset_ref[0]
    angles = position.astype(jnp.float32) * freq_ref[...]
    sine = jnp.sin(angles)
    latent = kv_ref[:, :LAT].astype(jnp.float32)
    mean_square = jnp.mean(latent * latent, axis=-1, keepdims=True)
    normed = latent * lax.rsqrt(mean_square + epsilon) * gain_ref[...]
    for t in range(4):
        rows[t] = normed[:, 128 * t : 128 * (t + 1)].astype(jnp.bfloat16).astype(jnp.float32)
    rope = kv_ref[:, LAT:].astype(jnp.float32)
    rope = rotate_lanes(rope, jnp.cos(angles), jnp.where(lane % ROPE < ROPE // 2, -sine, sine), lane)
    rows[4] = rope.astype(jnp.bfloat16).astype(jnp.float32)
    half = BLK // 2
    left = lax.broadcasted_iota(jnp.int32, (half, 128), 1) < ROPE
    for i in range(2):
        even = [rows[t, pl.ds(i * BLK, half, stride=2), :] for t in range(5)]
        odd = [pltpu.roll(rows[t, pl.ds(i * BLK + 1, half, stride=2), :], ROPE, 1) for t in range(5)]
        for t in range(9):
            if t < 4:
                tile = even[t]
            elif t == 4:
                tile = jnp.where(left, even[4], odd[0])
            else:
                tile = jnp.where(left, odd[t - 5], odd[t - 4])
            page[pl.ds(t, half, stride=9), :] = tile
        o_ref[i] = page[...].astype(jnp.bfloat16)


def make_pages(context, order_row, offsets, kv, gain):
    half = ROPE // 2
    lane = jnp.arange(128) % half
    freq = jnp.exp(-math.log(theta_base) * lane.astype(jnp.float32) / half)
    return pl.pallas_call(
        pages_kernel,
        in_specs=[SMEM] * 3 + [VMEM] * 3,
        out_specs=VMEM,
        out_shape=jax.ShapeDtypeStruct((2, PAGE, 128), jnp.bfloat16),
        scratch_shapes=[pltpu.VMEM((5, LOCAL, 128), jnp.float32), pltpu.VMEM((PAGE, 128), jnp.float32)],
        compiler_params=params(8),
        name="pages",
    )(context, order_row, offsets, kv, gain, freq[None])


def relay_kernel(req_ref, owners_ref, *refs):
    parts, outs, (table, count, sems) = refs[:4], refs[4:8], refs[8:]
    me = req_ref[0]
    my_x, my_z, my_core = me // 8, (me // 2) % 4, me % 2
    for i in range(16):
        table[i] = -1
    for i in range(8):
        count[i] = 0
    for z in range(4):
        for page in range(2):
            owner = owners_ref[page, request(my_x, z, my_core)]

            @pl.when((owner // 2) % 4 == my_z)
            def _():
                where = 2 * ((owner // 8 + 4 - my_x) % 4) + ((owner % 2) ^ my_core)
                slot = count[where]
                table[2 * where + jnp.minimum(slot, 1)] = 2 * ((my_z + 4 - z) % 4) + page
                count[where] = slot + 1

    def move(i, d):
        return pltpu.make_async_copy(parts[d].at[jnp.maximum(table[i], 0) % 2], outs[i // 4].at[i % 4], sems.at[i])

    for i in range(16):
        for d in range(4):

            @pl.when((table[i] >= 0) & (table[i] // 2 == d))
            def _():
                move(i, d).start()

    for i in range(16):

        @pl.when(table[i] >= 0)
        def _():
            move(i, 0).wait()


def relay_pages(req, owners, parts):
    page = parts[0].shape[1:]
    return pl.pallas_call(
        relay_kernel,
        in_specs=[SMEM, SMEM] + [ANY] * 4,
        out_specs=[VMEM] * 4,
        out_shape=[jax.ShapeDtypeStruct((4,) + page, parts[0].dtype)] * 4,
        scratch_shapes=[
            pltpu.SMEM((16,), jnp.int32),
            pltpu.SMEM((8,), jnp.int32),
            pltpu.SemaphoreType.DMA((16,)),
        ],
        compiler_params=params(8),
        name="relay_pages",
    )(req, owners, *parts)


def find(owner, target, my_x):
    flat = 2 * lax.broadcasted_iota(jnp.int32, owner.shape, 1) + lax.broadcasted_iota(jnp.int32, owner.shape, 0)
    last = jnp.max(jnp.where(owner == target, flat, 0))
    first = jnp.minimum(jnp.min(jnp.where(owner == target, flat, 4 * owner.shape[1])), last)
    found = []
    for page in (first, last):
        source = page // 2
        found.append(((my_x + 4 - source // 8) % 4, source % 2))
    same = (found[0][0] == found[1][0]) & (found[0][1] == found[1][1])
    return [found[0] + (0,), found[1] + (jnp.where(same, 1, 0),)]


def cross_kernel(req_ref, owners_ref, *refs):
    parts, o_ref = refs[:4], refs[4]
    me = req_ref[0]
    for i, (turn, core, slot) in enumerate(find(owners_ref[...], me ^ 1, me // 8)):
        for d, part in enumerate(parts):

            @pl.when((core == me % 2) & (turn == d))
            def _():
                o_ref[i] = part[2 + slot]


def keep_kernel(req_ref, owners_ref, crossed_ref, *refs):
    parts, o_ref = refs[:4], refs[4]
    me = req_ref[0]
    for i, (turn, core, slot) in enumerate(find(owners_ref[...], me, me // 8)):
        for d, part in enumerate(parts):

            @pl.when((core == me % 2) & (turn == d))
            def _():
                o_ref[i] = part[slot]

        @pl.when(core != me % 2)
        def _():
            o_ref[i] = crossed_ref[i]


def choose(kernel, req, owners, parts):
    return pl.pallas_call(
        kernel,
        in_specs=[SMEM] + [VMEM] * (1 + len(parts)),
        out_specs=VMEM,
        out_shape=jax.ShapeDtypeStruct((2,) + parts[0].shape[1:], parts[0].dtype),
        compiler_params=params(8),
    )(req, owners, *parts)


def request(x, z, core):
    return (x * 4 + z) * 2 + core


EACH = [(x, z, c) for x in range(4) for z in range(4) for c in range(2)]


def along_x(d):
    return [(request(x, z, c), request((x + d) % 4, z, c)) for x, z, c in EACH]


def along_z(d):
    return [(request(x, z, c), request(x, (z + d) % 4, c)) for x, z, c in EACH]


def ship(pages, owners):
    req, owners = lax.axis_index("req").reshape(1), owners.T
    parts = [pages] + [lax.ppermute(pages, "req", along_z(d)) for d in (1, 2, 3)]
    outgoing = relay_pages(req, owners, parts)
    parts = [outgoing[0]] + [lax.ppermute(outgoing[d], "req", along_x(d)) for d in (1, 2, 3)]
    crossing = choose(cross_kernel, req, owners, parts)
    crossed = lax.ppermute(crossing, "req", [(request(x, z, c), request(x, z, 1 - c)) for x, z, c in EACH])
    return choose(keep_kernel, req, owners, [crossed] + parts)


def exchange(array):
    return lax.all_to_all(array, "ctx", split_axis=0, concat_axis=0, tiled=True)


def body(q_heads, kv_latent, latent_gain, kv_up, offsets, lengths, block_order, owners):
    context = lax.axis_index("ctx").reshape(1)
    order_row = block_order[0]
    gain = latent_gain[None]
    padded = jnp.pad(kv_latent[0], ((0, 0), (0, KVP - kv_latent.shape[2])))
    beyond = lax.ppermute(padded, "ctx", forward(3))

    sent = pack(context, q_heads, 0, (0,) + EARLY)
    pages = make_pages(context, order_row, offsets, padded, gain)
    shipped = ship(pages, owners).reshape(1, 2, PAGE * 128)
    sent.update(pack(context, q_heads, 0, LATE, (padded, beyond)))
    arrived = [[sent[0]] + [lax.ppermute(sent[k], "ctx", forward(k)) for k in range(1, GROUPS)]]
    for chunk in range(1, CHUNKS):
        arrived.append([exchange(pack_all(chunk, q_heads))])
    offsets, _ = lax.optimization_barrier((offsets, sent[1]))
    lane = jnp.arange(128, dtype=jnp.int32)
    half = ROPE // 2
    frequency = jnp.exp(-math.log(theta_base) * (lane % half).astype(jnp.float32) / half)
    positions = offsets[0] + jnp.arange(GROUPS * LOCAL, dtype=jnp.int32)
    angles = positions.astype(jnp.float32)[:, None] * frequency[None, :]
    sign = jnp.where(lane % ROPE < half, -1.0, 1.0)
    extra = [jnp.cos(angles), jnp.sin(angles) * sign[None, :], gain, padded, beyond]
    attn_out = None
    for chunk in range(CHUNKS):
        out, kept = attend(chunk, context, order_row, lengths, arrived[chunk], kv_up, extra)
        extra = extra[:2] + list(kept) if chunk == 0 else extra
        attn_out = unpack(chunk, exchange(out), attn_out)
    return attn_out, shipped


def solution(mesh):
    in_specs = (
        P("req", "ctx", None),
        P("req", "ctx", None),
        P(),
        P("ctx", None, None),
        P("req"),
        P("req"),
        P("req", None),
        P(None, "ctx"),
    )
    out_specs = (P("req", "ctx", None), P("req", "ctx", None))
    return jax.shard_map(body, mesh=mesh, in_specs=in_specs, out_specs=out_specs, check_vma=False)
```

```python
import functools
import math

import jax
import jax.numpy as jnp
from jax import lax
from jax.experimental import pallas as pl
from jax.experimental.pallas import tpu as pltpu
from jax.sharding import PartitionSpec as P


HEADS = 64
HD = 128
ROPE = 64
LAT = 512
QW = HD + ROPE
PAIR = 2 * QW
BLK = 64
TILE = 256
GROUPS = 8
LOCAL = 2 * BLK
KVP = LAT + 128
PAGE = BLK * (LAT + ROPE) // 128

CHUNKS = 2
PAIRS = 4 // CHUNKS
QPART = PAIRS * PAIR
OPART = PAIRS * 2 * HD

theta_base = 10000.0
epsilon = 1e-06
masked_fill = -1e30
log2_scale = math.log2(math.e) * QW ** (-0.5)


NT = (((1,), (1,)), ((), ()))
SMEM = pl.BlockSpec(memory_space=pltpu.SMEM)
VMEM = pl.BlockSpec(memory_space=pltpu.VMEM)
ANY = pl.BlockSpec(memory_space=pl.ANY)

OFFSETS = ((0, 0), (0, 1), (0, 3), (1, 0), (1, 1), (1, 3), (0, 2), (1, 2))
BESIDE = {1: 4, 2: 5, 6: 7}
EARLY, LATE = (7, 4, 5, 3), (6, 1, 2)


def partner(context, k, back=False):
    dz, dy = OFFSETS[k]
    z, y = context // 4, context % 4
    step = 4 - dy if back else dy
    return ((z + dz) % 2) * 4 + (y + step) % 4


def forward(k):
    return [(d, partner(d, k)) for d in range(GROUPS)]


def backward(k):
    return [(partner(d, k), d) for d in range(GROUPS)]


def params(limit):
    return pltpu.CompilerParams(vmem_limit_bytes=limit << 20)


def rotate_lanes(x, cosine, sine, lane):
    half = ROPE // 2
    swapped = jnp.where(lane % ROPE < half, pltpu.roll(x, 128 - half, 1), pltpu.roll(x, half, 1))
    return x * cosine + swapped * sine


def pack_kernel(chunk, partners, n_kv, *refs):
    ctx_ref, q_ref, *refs = refs
    kvs, refs = refs[:n_kv], refs[n_kv:]
    outs, (held, sems) = refs[: len(partners)], refs[len(partners) :]
    loads, stores = [], []
    for n, k in enumerate(partners):
        column = partner(ctx_ref[0], k) * (4 * PAIR) + chunk * QPART
        columns = pl.ds(pl.multiple_of(column, 128), QPART)
        loads.append(pltpu.make_async_copy(q_ref.at[0, :, columns], held.at[n], sems.at[0, n]))
        loads[-1].start()
    for n in range(len(partners)):
        for i, kv in enumerate(kvs):
            columns = pl.ds(QPART + i * KVP, KVP)
            stores.append(pltpu.make_async_copy(kv, outs[n].at[:, columns], sems.at[2 + i, n]))
            stores[-1].start()
    for n in range(len(partners)):
        loads[n].wait()
        stores.append(pltpu.make_async_copy(held.at[n], outs[n].at[:, :QPART], sems.at[1, n]))
        stores[-1].start()
    for store in stores:
        store.wait()


def pack(context, q_heads, chunk, partners, kvs=()):
    count = len(partners)
    outs = pl.pallas_call(
        functools.partial(pack_kernel, chunk, partners, len(kvs)),
        in_specs=[SMEM, ANY] + [VMEM] * len(kvs),
        out_specs=[ANY] * count,
        out_shape=[jax.ShapeDtypeStruct((LOCAL, QPART + len(kvs) * KVP), jnp.bfloat16)] * count,
        scratch_shapes=[
            pltpu.VMEM((count, LOCAL, QPART), jnp.bfloat16),
            pltpu.SemaphoreType.DMA((4, count)),
        ],
        compiler_params=params(8 if kvs else 60),
        name="pack",
    )(context, q_heads, *kvs)
    return dict(zip(partners, outs))


def pack_all_kernel(chunk, q_ref, o_ref, held, sems):
    loads, stores = [], []
    for j in range(GROUPS):
        columns = pl.ds(j * (4 * PAIR) + chunk * QPART, QPART)
        loads.append(pltpu.make_async_copy(q_ref.at[0, :, columns], held.at[j], sems.at[0, j]))
        loads[-1].start()
    for j in range(GROUPS):
        loads[j].wait()
        stores.append(pltpu.make_async_copy(held.at[j], o_ref.at[j], sems.at[1, j]))
        stores[-1].start()
    for store in stores:
        store.wait()


def pack_all(chunk, q_heads):
    shape = (GROUPS, LOCAL, QPART)
    return pl.pallas_call(
        functools.partial(pack_all_kernel, chunk),
        in_specs=[ANY],
        out_specs=ANY,
        out_shape=jax.ShapeDtypeStruct(shape, jnp.bfloat16),
        scratch_shapes=[pltpu.VMEM(shape, jnp.bfloat16), pltpu.SemaphoreType.DMA((2, GROUPS))],
        compiler_params=params(60),
        name="pack_all",
    )(q_heads)


def attend_kernel(chunk, *refs):
    first = chunk == 0
    ctx_ref, order_ref, length_ref, *refs = refs
    if first:
        arrived, refs = refs[:GROUPS], refs[GROUPS:]
        w_hbm, cos_hbm, sin_hbm, gain_ref, kv_hbm, kvz_hbm, o_ref, cs_hbm, krl_hbm, krr_hbm, *refs = refs
    else:
        stacked, w_hbm, cos_hbm, sin_hbm, cs_hbm, krl_hbm, krr_hbm, *refs = refs
        outs, refs = refs[:GROUPS], refs[GROUPS:]
        arrived = [stacked.at[k] for k in range(GROUPS)]
    w_ref, cs, krl, krr, cos_ref, sin_ref, qs, os, k0, k1, v, sems, out_sems = refs
    total = cs.shape[0]
    context = ctx_ref[0]
    started = []

    def load(source, target):
        copy = pltpu.make_async_copy(source, target, sems.at[len(started)])
        copy.start()
        started.append(copy)
        return copy

    rows_of = {}
    if first:
        rows_of = {0: (kv_hbm, 0), 3: (kvz_hbm, 0)}
        for k, beyond in BESIDE.items():
            rows_of[k] = (arrived[k], QPART)
            rows_of[beyond] = (arrived[k], QPART + KVP)
    places, moves = [], []
    for k in range(GROUPS):
        source = partner(context, k, back=True) if first else k
        for i in range(2):
            place = pl.multiple_of(order_ref[2 * source + i] * BLK, BLK)
            places.append((2 * source + i, place))
            moves.append((k, pl.ds(i * BLK, BLK), pl.ds(place, BLK)))
    targets = []
    for n, (block, place) in enumerate(places):
        if first:
            targets.append((place, o_ref.at[block]))
        else:
            k, i = n // 2, n % 2
            place = pl.multiple_of(order_ref[2 * partner(context, k, back=True) + i] * BLK, BLK)
            targets.append((place, outs[k].at[pl.ds(i * BLK, BLK)]))
    keys_here = []
    if first:
        for k, here, there in moves:
            ref, at = rows_of[k]
            keys_here.append(load(ref.at[here, pl.ds(at, LAT)], cs.at[there]))
            keys_here.append(load(ref.at[here, pl.ds(at + LAT, KVP - LAT)], krl.at[there]))
    else:
        keys_here = [load(cs_hbm, cs), load(krl_hbm, krl), load(krr_hbm, krr)]
    tables_here = [load(cos_hbm, cos_ref), load(sin_hbm, sin_ref)]
    weights_here, queries_here = [], []
    for pair in range(PAIRS):
        heads = pl.ds(2 * (chunk * PAIRS + pair), 2)
        weights_here.append(load(w_hbm.at[heads], w_ref.at[pl.ds(2 * pair, 2)]))
        queries_here.append(
            [load(arrived[k].at[here, pl.ds(pair * PAIR, PAIR)], qs.at[pair, there]) for k, here, there in moves]
        )
    for copy in keys_here + tables_here * first:
        copy.wait()

    lane = lax.broadcasted_iota(jnp.int32, (TILE, 128), 1)
    if first:
        for t in range(total // TILE):
            rows = slice(t * TILE, (t + 1) * TILE)
            latent = cs[rows, :].astype(jnp.float32)
            mean_square = jnp.mean(latent * latent, axis=-1, keepdims=True)
            cs[rows, :] = (latent * lax.rsqrt(mean_square + epsilon) * gain_ref[...]).astype(jnp.bfloat16)
            turned = rotate_lanes(krl[rows, :].astype(jnp.float32), cos_ref[rows, :], sin_ref[rows, :], lane)
            krl[rows, :] = turned.astype(jnp.bfloat16)
            krr[rows, :] = pltpu.roll(turned, ROPE, 1).astype(jnp.bfloat16)
    kept = [load(cs, cs_hbm), load(krl, krl_hbm), load(krr, krr_hbm)] if first else []
    length = length_ref[0]

    row = lax.broadcasted_iota(jnp.int32, (TILE, TILE), 0)
    column = lax.broadcasted_iota(jnp.int32, (TILE, TILE), 1)
    stores = []

    def project(pair):
        gap = jnp.zeros((ROPE, LAT), jnp.bfloat16)
        w0, w1 = w_ref[2 * pair], w_ref[2 * pair + 1]
        wk = jnp.concatenate([w0[:HD], gap, w1[:HD], gap], axis=0)
        wv = jnp.concatenate([w0[HD:], w1[HD:]], axis=0)
        for t in range(total // TILE):
            rows = slice(t * TILE, (t + 1) * TILE)
            cache = cs[rows, :]
            kn = lax.dot_general(cache, wk, NT, preferred_element_type=jnp.float32).astype(jnp.bfloat16)
            k0[pair, rows, :128] = kn[:, :128]
            k0[pair, rows, 128:] = krl[rows, :]
            k1[pair, rows, :128] = kn[:, 128:256]
            k1[pair, rows, 128:] = kn[:, 256:] + krr[rows, :]
            v[pair, rows, :] = lax.dot_general(cache, wv, NT, preferred_element_type=jnp.float32).astype(jnp.bfloat16)

    def score(pair, t, head):
        rows = slice(t * TILE, (t + 1) * TILE)
        cosine, sine = cos_ref[rows, :], sin_ref[rows, :]
        mixed = qs[pair, rows, 128 * (1 + head) : 128 * (2 + head)].astype(jnp.float32)
        turned = rotate_lanes(mixed, cosine, sine, lane)
        if head == 0:
            mixed = jnp.where(lane < ROPE, turned, mixed).astype(jnp.bfloat16)
            query = jnp.concatenate([qs[pair, rows, :128], mixed], axis=1)
        else:
            mixed = jnp.where(lane < ROPE, mixed, turned).astype(jnp.bfloat16)
            query = jnp.concatenate([qs[pair, rows, 128:256], mixed], axis=1)
        k = (k0, k1)[head]
        last = lax.dot_general(query, k[pair, rows, :], NT, preferred_element_type=jnp.float32)
        last = jnp.where(column <= row, last, masked_fill)
        if t == 0:
            return [last]
        return [lax.dot_general(query, k[pair, : t * TILE, :], NT, preferred_element_type=jnp.float32), last]

    def weigh(pair, t, head, scores):
        rows = slice(t * TILE, (t + 1) * TILE)
        side = slice(head * HD, (head + 1) * HD)
        valid = lax.broadcasted_iota(jnp.int32, (TILE, HD), 0) + t * TILE < length
        top = functools.reduce(jnp.maximum, [jnp.max(s, axis=1, keepdims=True) for s in scores])
        parts = [jnp.exp2((s - top) * log2_scale) for s in scores]
        bottom = functools.reduce(jnp.add, [jnp.sum(p, axis=1, keepdims=True) for p in parts])
        values = [v[pair, : t * TILE, side], v[pair, rows, side]][-len(parts) :]
        o = functools.reduce(
            jnp.add,
            [jnp.dot(p.astype(jnp.bfloat16), u, preferred_element_type=jnp.float32) for p, u in zip(parts, values)],
        )
        os[pair, rows, side] = jnp.where(valid, o / bottom, 0.0).astype(jnp.bfloat16)

    for pair in range(PAIRS):
        weights_here[pair].wait()
        project(pair)
        for copy in queries_here[pair] + tables_here * (not first and pair == 0):
            copy.wait()
        items = [(t, head) for t in range(total // TILE) for head in range(2)]
        ahead = score(pair, *items[0])
        for n, item in enumerate(items):
            scores = ahead
            if n + 1 < len(items):
                ahead = score(pair, *items[n + 1])
            weigh(pair, *item, scores)
        columns = pl.ds(pair * (2 * HD), 2 * HD)
        for n, (place, target) in enumerate(targets):
            stores.append(
                pltpu.make_async_copy(os.at[pair, pl.ds(place, BLK)], target.at[:, columns], out_sems.at[pair, n])
            )
            stores[-1].start()
    for copy in stores + kept:
        copy.wait()


def attend(chunk, context, order_row, length, arrived, kv_up, extra):
    first = chunk == 0
    total = GROUPS * LOCAL
    if first:
        shapes = [(2 * GROUPS, BLK, OPART), (total, LAT), (total, 128), (total, 128)]
    else:
        shapes = [(LOCAL, OPART)] * GROUPS
    n_arrived = len(arrived)
    sides = [ANY, ANY, VMEM, ANY, ANY] if first else [ANY] * 5
    outs = pl.pallas_call(
        functools.partial(attend_kernel, chunk),
        in_specs=[SMEM, SMEM, SMEM] + [ANY] * (n_arrived + 1) + sides,
        out_specs=[ANY] * len(shapes),
        out_shape=[jax.ShapeDtypeStruct(shape, jnp.bfloat16) for shape in shapes],
        scratch_shapes=[
            pltpu.VMEM((2 * PAIRS, 2 * HD, LAT), jnp.bfloat16),
            pltpu.VMEM((total, LAT), jnp.bfloat16),
            pltpu.VMEM((total, 128), jnp.bfloat16),
            pltpu.VMEM((total, 128), jnp.bfloat16),
            pltpu.VMEM((total, 128), jnp.float32),
            pltpu.VMEM((total, 128), jnp.float32),
            pltpu.VMEM((PAIRS, total, PAIR), jnp.bfloat16),
            pltpu.VMEM((PAIRS, total, 2 * HD), jnp.bfloat16),
            pltpu.VMEM((PAIRS, total, 256), jnp.bfloat16),
            pltpu.VMEM((PAIRS, total, 256), jnp.bfloat16),
            pltpu.VMEM((PAIRS, total, 256), jnp.bfloat16),
            pltpu.SemaphoreType.DMA((7 + (2 + PAIRS) * 2 * GROUPS,)),
            pltpu.SemaphoreType.DMA((PAIRS, 2 * GROUPS)),
        ],
        compiler_params=params(60),
        cost_estimate=pl.CostEstimate(
            flops=PAIRS * 2_200_000_000, bytes_accessed=6_000_000, transcendentals=PAIRS * 1_300_000
        ),
        name="attend",
    )(context, order_row, length, *arrived, kv_up, *extra)
    if first:
        return outs[0].reshape(GROUPS, LOCAL, OPART), outs[1:]
    return outs, ()


def unpack_kernel(chunk, ctx_ref, *refs):
    o_ref, sems = refs[-2:]
    stores = []
    for n in range(GROUPS):
        if chunk == 0:
            part, group = refs[0].at[n], n
        else:
            part, group = refs[n], partner(ctx_ref[0], n)
        columns = pl.ds(pl.multiple_of(group * (8 * HD) + chunk * OPART, 128), OPART)
        stores.append(pltpu.make_async_copy(part, o_ref.at[0, :, columns], sems.at[n]))
        stores[-1].start()
    for store in stores:
        store.wait()


def unpack(chunk, context, parts, out):
    more = [] if out is None else [out]
    return pl.pallas_call(
        functools.partial(unpack_kernel, chunk),
        in_specs=[SMEM] + [VMEM] * len(parts) + [ANY] * len(more),
        out_specs=ANY,
        out_shape=jax.ShapeDtypeStruct((1, LOCAL, HEADS * HD), jnp.bfloat16),
        scratch_shapes=[pltpu.SemaphoreType.DMA((GROUPS,))],
        input_output_aliases={1 + len(parts): 0} if more else {},
        compiler_params=params(8),
        name="unpack",
    )(context, *parts, *more)


def pages_kernel(ctx_ref, order_ref, offset_ref, kv_ref, gain_ref, freq_ref, o_ref, rows, page):
    row = lax.broadcasted_iota(jnp.int32, (LOCAL, 128), 0)
    lane = lax.broadcasted_iota(jnp.int32, (LOCAL, 128), 1)
    first, second = order_ref[2 * ctx_ref[0]], order_ref[2 * ctx_ref[0] + 1]
    position = jnp.where(row < BLK, first, second) * BLK + row % BLK + offset_ref[0]
    angles = position.astype(jnp.float32) * freq_ref[...]
    sine = jnp.sin(angles)
    latent = kv_ref[:, :LAT].astype(jnp.float32)
    mean_square = jnp.mean(latent * latent, axis=-1, keepdims=True)
    normed = latent * lax.rsqrt(mean_square + epsilon) * gain_ref[...]
    for t in range(4):
        rows[t] = normed[:, 128 * t : 128 * (t + 1)].astype(jnp.bfloat16).astype(jnp.float32)
    rope = kv_ref[:, LAT:].astype(jnp.float32)
    rope = rotate_lanes(rope, jnp.cos(angles), jnp.where(lane % ROPE < ROPE // 2, -sine, sine), lane)
    rows[4] = rope.astype(jnp.bfloat16).astype(jnp.float32)
    half = BLK // 2
    left = lax.broadcasted_iota(jnp.int32, (half, 128), 1) < ROPE
    for i in range(2):
        even = [rows[t, pl.ds(i * BLK, half, stride=2), :] for t in range(5)]
        odd = [pltpu.roll(rows[t, pl.ds(i * BLK + 1, half, stride=2), :], ROPE, 1) for t in range(5)]
        for t in range(9):
            if t < 4:
                tile = even[t]
            elif t == 4:
                tile = jnp.where(left, even[4], odd[0])
            else:
                tile = jnp.where(left, odd[t - 5], odd[t - 4])
            page[pl.ds(t, half, stride=9), :] = tile
        o_ref[i] = page[...].astype(jnp.bfloat16)


def make_pages(context, order_row, offsets, kv, gain):
    half = ROPE // 2
    lane = jnp.arange(128) % half
    freq = jnp.exp(-math.log(theta_base) * lane.astype(jnp.float32) / half)
    return pl.pallas_call(
        pages_kernel,
        in_specs=[SMEM] * 3 + [VMEM] * 3,
        out_specs=VMEM,
        out_shape=jax.ShapeDtypeStruct((2, PAGE, 128), jnp.bfloat16),
        scratch_shapes=[pltpu.VMEM((5, LOCAL, 128), jnp.float32), pltpu.VMEM((PAGE, 128), jnp.float32)],
        compiler_params=params(8),
        name="pages",
    )(context, order_row, offsets, kv, gain, freq[None])


def relay_kernel(req_ref, owners_ref, *refs):
    parts, outs, (table, count, sems) = refs[:4], refs[4:8], refs[8:]
    me = req_ref[0]
    my_x, my_z, my_core = me // 8, (me // 2) % 4, me % 2
    for i in range(16):
        table[i] = -1
    for i in range(8):
        count[i] = 0
    for z in range(4):
        for page in range(2):
            owner = owners_ref[page, request(my_x, z, my_core)]

            @pl.when((owner // 2) % 4 == my_z)
            def _():
                where = 2 * ((owner // 8 + 4 - my_x) % 4) + ((owner % 2) ^ my_core)
                slot = count[where]
                table[2 * where + jnp.minimum(slot, 1)] = 2 * ((my_z + 4 - z) % 4) + page
                count[where] = slot + 1

    def move(i, d):
        return pltpu.make_async_copy(parts[d].at[jnp.maximum(table[i], 0) % 2], outs[i // 4].at[i % 4], sems.at[i])

    for i in range(16):
        for d in range(4):

            @pl.when((table[i] >= 0) & (table[i] // 2 == d))
            def _():
                move(i, d).start()

    for i in range(16):

        @pl.when(table[i] >= 0)
        def _():
            move(i, 0).wait()


def relay_pages(req, owners, parts):
    page = parts[0].shape[1:]
    return pl.pallas_call(
        relay_kernel,
        in_specs=[SMEM, SMEM] + [ANY] * 4,
        out_specs=[VMEM] * 4,
        out_shape=[jax.ShapeDtypeStruct((4,) + page, parts[0].dtype)] * 4,
        scratch_shapes=[
            pltpu.SMEM((16,), jnp.int32),
            pltpu.SMEM((8,), jnp.int32),
            pltpu.SemaphoreType.DMA((16,)),
        ],
        compiler_params=params(8),
        name="relay_pages",
    )(req, owners, *parts)


def find(owner, target, my_x):
    flat = 2 * lax.broadcasted_iota(jnp.int32, owner.shape, 1) + lax.broadcasted_iota(jnp.int32, owner.shape, 0)
    last = jnp.max(jnp.where(owner == target, flat, 0))
    first = jnp.minimum(jnp.min(jnp.where(owner == target, flat, 4 * owner.shape[1])), last)
    found = []
    for page in (first, last):
        source = page // 2
        found.append(((my_x + 4 - source // 8) % 4, source % 2))
    same = (found[0][0] == found[1][0]) & (found[0][1] == found[1][1])
    return [found[0] + (0,), found[1] + (jnp.where(same, 1, 0),)]


def cross_kernel(req_ref, owners_ref, *refs):
    parts, o_ref = refs[:4], refs[4]
    me = req_ref[0]
    for i, (turn, core, slot) in enumerate(find(owners_ref[...], me ^ 1, me // 8)):
        for d, part in enumerate(parts):

            @pl.when((core == me % 2) & (turn == d))
            def _():
                o_ref[i] = part[2 + slot]


def keep_kernel(req_ref, owners_ref, crossed_ref, *refs):
    parts, o_ref = refs[:4], refs[4]
    me = req_ref[0]
    for i, (turn, core, slot) in enumerate(find(owners_ref[...], me, me // 8)):
        for d, part in enumerate(parts):

            @pl.when((core == me % 2) & (turn == d))
            def _():
                o_ref[i] = part[slot]

        @pl.when(core != me % 2)
        def _():
            o_ref[i] = crossed_ref[i]


def choose(kernel, req, owners, parts):
    return pl.pallas_call(
        kernel,
        in_specs=[SMEM] + [VMEM] * (1 + len(parts)),
        out_specs=VMEM,
        out_shape=jax.ShapeDtypeStruct((2,) + parts[0].shape[1:], parts[0].dtype),
        compiler_params=params(8),
    )(req, owners, *parts)


def request(x, z, core):
    return (x * 4 + z) * 2 + core


EACH = [(x, z, c) for x in range(4) for z in range(4) for c in range(2)]


def along_x(d):
    return [(request(x, z, c), request((x + d) % 4, z, c)) for x, z, c in EACH]


def along_z(d):
    return [(request(x, z, c), request(x, (z + d) % 4, c)) for x, z, c in EACH]


def ship(pages, owners):
    req, owners = lax.axis_index("req").reshape(1), owners.T
    parts = [pages] + [lax.ppermute(pages, "req", along_z(d)) for d in (1, 2, 3)]
    outgoing = relay_pages(req, owners, parts)
    parts = [outgoing[0]] + [lax.ppermute(outgoing[d], "req", along_x(d)) for d in (1, 2, 3)]
    crossing = choose(cross_kernel, req, owners, parts)
    crossed = lax.ppermute(crossing, "req", [(request(x, z, c), request(x, z, 1 - c)) for x, z, c in EACH])
    return choose(keep_kernel, req, owners, [crossed] + parts)


def exchange(array):
    return lax.all_to_all(array, "ctx", split_axis=0, concat_axis=0, tiled=True)


def body(q_heads, kv_latent, latent_gain, kv_up, offsets, lengths, block_order, owners):
    context = lax.axis_index("ctx").reshape(1)
    order_row = block_order[0]
    gain = latent_gain[None]
    padded = jnp.pad(kv_latent[0], ((0, 0), (0, KVP - kv_latent.shape[2])))
    beyond = lax.ppermute(padded, "ctx", forward(3))

    sent = pack(context, q_heads, 0, (0,) + EARLY)
    pages = make_pages(context, order_row, offsets, padded, gain)
    shipped = ship(pages, owners).reshape(1, 2, PAGE * 128)
    sent.update(pack(context, q_heads, 0, LATE, (padded, beyond)))
    arrived = [[sent[0]] + [lax.ppermute(sent[k], "ctx", forward(k)) for k in range(1, GROUPS)]]
    for chunk in range(1, CHUNKS):
        arrived.append([exchange(pack_all(chunk, q_heads))])
    offsets, _ = lax.optimization_barrier((offsets, sent[1]))
    lane = jnp.arange(128, dtype=jnp.int32)
    half = ROPE // 2
    frequency = jnp.exp(-math.log(theta_base) * (lane % half).astype(jnp.float32) / half)
    positions = offsets[0] + jnp.arange(GROUPS * LOCAL, dtype=jnp.int32)
    angles = positions.astype(jnp.float32)[:, None] * frequency[None, :]
    sign = jnp.where(lane % ROPE < half, -1.0, 1.0)
    extra = [jnp.cos(angles), jnp.sin(angles) * sign[None, :], gain, padded, beyond]
    attn_out = None
    for chunk in range(CHUNKS):
        out, kept = attend(chunk, context, order_row, lengths, arrived[chunk], kv_up, extra)
        extra = extra[:2] + list(kept) if chunk == 0 else extra
        if chunk == 0:
            parts = [exchange(out)]
        else:
            parts = [out[0]] + [lax.ppermute(out[k], "ctx", backward(k)) for k in range(1, GROUPS)]
        attn_out = unpack(chunk, context, parts, attn_out)
    return attn_out, shipped


def solution(mesh):
    in_specs = (
        P("req", "ctx", None),
        P("req", "ctx", None),
        P(),
        P("ctx", None, None),
        P("req"),
        P("req"),
        P("req", None),
        P(None, "ctx"),
    )
    out_specs = (P("req", "ctx", None), P("req", "ctx", None))
    return jax.shard_map(body, mesh=mesh, in_specs=in_specs, out_specs=out_specs, check_vma=False)
```
